1024 devices in a mesh: seq: 32 (over x, z_hi), head: 32 (over y, z_lo, core).
Axes of the slice: x: 8, y: 8, z: 8 (z_hi: 4, z_lo: 2; z = z_hi * 2 + z_lo), core: 2. Of those that a mesh axis runs over, the one named last changes fastest.
Arguments:
- inputs: bfloat16 [24576, 8192], P('seq', 'head'), may hold values from -6 to 6
- log_decay: float32 [128, 24576], P('head', 'seq'), may hold values from -3 to 0, as said below
- write_proj: bfloat16 [24576, 128], P('seq'), may hold values from -0.5 to 0.5
- read_proj: bfloat16 [24576, 128], P('seq'), may hold values from -0.5 to 0.5
- grad_out: bfloat16 [24576, 8192], P('seq', 'head'), may hold values from -0.75 to 0.75
Outputs:
- outputs: bfloat16 [24576, 8192], P('seq', 'head')
- grad_inputs: bfloat16 [24576, 8192], P('seq', 'head')
- grad_write: float32 [24576, 128], P(('seq', 'head'))
- grad_read: float32 [24576, 128], P(('seq', 'head'))
The draws below stay inside these ranges and needn't reach their ends.
Inputs may be any that keep to these rules, and one draw needn't show every extreme that they name: log_decay is negative everywhere.
All inputs are finite; a program needn't handle non-finite values.
Results may differ from the reference program's by a relative error of at most 0.0032.
Values sent between devices are 32-bit elements; how exact they have to be, the bound alone decides.
No kernel may reach another device: no remote copies, remote signals or barrier semaphores. Data moves between devices by JAX's collectives and lax.ppermute only.
A program may use at most 64 MiB of HBM per device.

```python
import jax
import jax.numpy as jnp
from jax import lax

MIXER_HEADS = 128
HEAD_DIM = 64
STATE = 128
TOK_DEV = 768
SEQUENCE_TOKENS = 24576
INNER = 8192


def draw_log_decay(key, part):
    random_keys = jax.random.split(jax.random.fold_in(key, 17), 7)
    fast_share = 0.5
    is_fast = jax.random.uniform(random_keys[0], (MIXER_HEADS, 1)) < fast_share
    fast_rate = 1.0 / jax.random.uniform(random_keys[1], (MIXER_HEADS, 1), minval=30.0, maxval=50.0)
    slow_rate = jax.random.uniform(random_keys[2], (MIXER_HEADS, 1), minval=0.2, maxval=0.6) / SEQUENCE_TOKENS
    decay_speed = jnp.where(is_fast, fast_rate, slow_rate)
    sections = SEQUENCE_TOKENS // TOK_DEV
    section_divisor = jnp.exp(jax.random.uniform(random_keys[3], (MIXER_HEADS, sections, 1), minval=-0.7, maxval=0.7))
    section_divisor = jnp.broadcast_to(section_divisor, (MIXER_HEADS, sections, TOK_DEV)).reshape(MIXER_HEADS, SEQUENCE_TOKENS)
    token_divisor = jnp.exp(jax.random.uniform(random_keys[4], (MIXER_HEADS, SEQUENCE_TOKENS), minval=-0.7, maxval=0.7))
    section_offset = jax.random.randint(random_keys[5], (MIXER_HEADS, 4), 0, SEQUENCE_TOKENS)
    section_length = jax.random.uniform(random_keys[6], (MIXER_HEADS, 4), minval=0.22, maxval=0.69)
    token_position = jnp.arange(SEQUENCE_TOKENS, dtype=jnp.int32)
    section_count = jnp.zeros((MIXER_HEADS, SEQUENCE_TOKENS), jnp.float32)
    for token_index in range(4):
        section_count = section_count + jnp.where(token_position[None, :] == section_offset[:, token_index:token_index + 1], section_length[:, token_index:token_index + 1], 0.0)
    return -(decay_speed * section_divisor * token_divisor + section_count)


def block_levels(rng, extent, pieces, smallest, top_value):
    level, own = 1.0, jax.random.fold_in(rng, 6)
    for dim, shards_of in pieces:
        steps = jnp.exp(jax.random.uniform(jax.random.fold_in(own, dim), (shards_of,), jnp.float32, smallest / len(pieces), top_value / len(pieces)))
        level = level * jnp.repeat(steps, extent[dim] // shards_of).reshape([-1 if axis == dim else 1 for axis in range(len(extent))])
    return level


def centred(rng, shape, deviation, bound, cuts=(), kind=jnp.bfloat16):
    gain = block_levels(rng, shape, cuts, -0.22, 0.18) if cuts else 1.0
    drawn = jax.random.normal(rng, shape, jnp.float32) * deviation * gain
    return jnp.minimum(jnp.maximum(drawn, -bound), bound).astype(kind)


def setup_inputs(seed: int = 0) -> dict:
    splits = jax.random.split(jax.random.key(seed), 6)
    return {
        "inputs": centred(splits[0], (SEQUENCE_TOKENS, INNER), 1.0, 6.0, ((0, 32), (1, 32))),
        "log_decay": draw_log_decay(jax.random.fold_in(splits[5], 71), 0),
        "write_proj": centred(splits[2], (SEQUENCE_TOKENS, STATE), STATE ** -0.5, 0.5, ((0, 32),)),
        "read_proj": centred(splits[3], (SEQUENCE_TOKENS, STATE), STATE ** -0.5, 0.5, ((0, 32),)),
        "grad_out": centred(splits[4], (SEQUENCE_TOKENS, INNER), 0.125, 0.75, ((0, 32), (1, 32))),
    }


highest = lax.Precision.HIGHEST


def section_states(items):
    x_part, g_part, write_part, read_part, decay_part = items
    cumulative = jnp.cumsum(decay_part, axis=1)
    last_cumul = cumulative[:, -1:]
    tail_weight = jnp.exp(last_cumul - cumulative)
    lead_weight = jnp.exp(cumulative)
    x_wide = x_part.astype(jnp.float32)
    g_wide = g_part.astype(jnp.float32)
    local_state = jnp.einsum("jhp,jn->hpn", x_wide * tail_weight.T[:, :, None], write_part.astype(jnp.float32), precision=highest)
    local_grad = jnp.einsum("thp,tn->hpn", g_wide * lead_weight.T[:, :, None], read_part.astype(jnp.float32), precision=highest)
    return jnp.exp(last_cumul[:, 0]), local_state, local_grad


def section_outputs(items):
    x_part, g_part, write_part, read_part, decay_part, state_in, grad_state = items
    length = x_part.shape[0]
    cumulative = jnp.cumsum(decay_part, axis=1)
    last_cumul = cumulative[:, -1:]
    tail_weight = jnp.exp(last_cumul - cumulative)
    lead_weight = jnp.exp(cumulative)
    rows_index = lax.broadcasted_iota(jnp.int32, (length, length), 0)
    cols_index = lax.broadcasted_iota(jnp.int32, (length, length), 1)
    causal = rows_index >= cols_index
    differ = cumulative[:, :, None] - cumulative[:, None, :]
    decay_mat = jnp.exp(jnp.where(causal[None], differ, -jnp.inf))
    scores = jnp.dot(read_part, write_part.T, preferred_element_type=jnp.float32)
    mixing = (scores[None] * decay_mat).astype(jnp.bfloat16).astype(jnp.float32)
    x_wide = x_part.astype(jnp.float32)
    g_wide = g_part.astype(jnp.float32)
    write_wide = write_part.astype(jnp.float32)
    read_wide = read_part.astype(jnp.float32)
    y_intra = jnp.einsum("htj,jhp->thp", mixing, x_wide, precision=highest)
    y_inter = jnp.einsum("tn,hpn->thp", read_wide, state_in, precision=highest) * lead_weight.T[:, :, None]
    outputs = (y_intra + y_inter).astype(jnp.bfloat16).reshape(length, -1)
    grad_prod = jnp.einsum("thp,jhp->htj", g_wide, x_wide, precision=highest)
    grad_score = jnp.sum(grad_prod * decay_mat, axis=0)
    dx_intra = jnp.einsum("htj,thp->jhp", mixing, g_wide, precision=highest)
    dx_inter = jnp.einsum("jn,hpn->jhp", write_wide, grad_state, precision=highest) * tail_weight.T[:, :, None]
    grad_inputs = (dx_intra + dx_inter).astype(jnp.bfloat16).reshape(length, -1)
    grad_write = jnp.dot(grad_score.T, read_wide, precision=highest) + jnp.einsum("jhp,hpn->jn", x_wide * tail_weight.T[:, :, None], grad_state, precision=highest)
    grad_read = jnp.dot(grad_score, write_wide, precision=highest) + jnp.einsum("thp,hpn->tn", g_wide * lead_weight.T[:, :, None], state_in, precision=highest)
    return outputs, grad_inputs, grad_write, grad_read


def carry_step(carry, item):
    total, local = item
    return total[:, None, None] * carry + local, carry


def reference(inputs, log_decay, write_proj, read_proj, grad_out):
    sections = SEQUENCE_TOKENS // TOK_DEV
    x_sec = inputs.reshape(sections, TOK_DEV, MIXER_HEADS, HEAD_DIM)
    g_sec = grad_out.reshape(sections, TOK_DEV, MIXER_HEADS, HEAD_DIM)
    write_sec = write_proj.reshape(sections, TOK_DEV, STATE)
    read_sec = read_proj.reshape(sections, TOK_DEV, STATE)
    decay_sec = log_decay.reshape(MIXER_HEADS, sections, TOK_DEV).transpose(1, 0, 2)
    totals, local_states, local_grads = lax.map(section_states, (x_sec, g_sec, write_sec, read_sec, decay_sec))
    zero_block = jnp.zeros((MIXER_HEADS, HEAD_DIM, STATE), jnp.float32)
    _, state_in = lax.scan(carry_step, zero_block, (totals, local_states))
    _, grad_state = lax.scan(carry_step, zero_block, (totals, local_grads), reverse=True)
    outputs, grad_inputs, grad_write, grad_read = lax.map(section_outputs, (x_sec, g_sec, write_sec, read_sec, decay_sec, state_in, grad_state))
    return (outputs.reshape(SEQUENCE_TOKENS, MIXER_HEADS * HEAD_DIM), grad_inputs.reshape(SEQUENCE_TOKENS, MIXER_HEADS * HEAD_DIM), grad_write.reshape(SEQUENCE_TOKENS, STATE), grad_read.reshape(SEQUENCE_TOKENS, STATE))
```

```python
import functools

import jax
import jax.numpy as jnp
from jax import lax
from jax.experimental import pallas as pl
from jax.experimental.pallas import tpu as pltpu
from jax.sharding import Mesh, PartitionSpec as P

f32 = jnp.float32
bf16 = jnp.bfloat16
VMEM = pl.BlockSpec(memory_space=pltpu.VMEM)
SMEM = pl.BlockSpec(memory_space=pltpu.SMEM)
BLOCK = 256


def dot(a, b, dims):
    return lax.dot_general(a, b, (dims, ((), ())), preferred_element_type=f32)


def split(value):
    high = value.astype(bf16)
    return high, (value - high.astype(f32)).astype(bf16)


def lanes_of_heads(columns, heads, width):
    tokens = columns.shape[0]
    lane = lax.broadcasted_iota(jnp.int32, (tokens, heads * width), 1) // width
    spread = jnp.broadcast_to(columns[:, 0:1], (tokens, heads * width))
    for head in range(1, heads):
        spread = jnp.where(lane == head, columns[:, head : head + 1], spread)
    return spread


def local_kernel(
    sections, x_ref, g_ref, write_ref, read_ref, decay_ref, send_ref, rows_ref, cols_ref, weights_ref
):
    heads, tokens = decay_ref.shape
    channels = x_ref.shape[1]
    head_size = channels // heads
    chunk = channels // sections
    decay = jnp.concatenate([decay_ref[...], jnp.zeros((8 - heads, tokens), f32)], axis=0)
    row_id = lax.broadcasted_iota(jnp.int32, (tokens, tokens), 0)
    col_id = lax.broadcasted_iota(jnp.int32, (tokens, tokens), 1)
    upto = (row_id <= col_id).astype(f32).astype(bf16)
    first, rest = split(decay)
    rest_wide = decay - first.astype(f32)
    second, third = split(rest_wide)
    pieces = jnp.concatenate([first.astype(f32), second.astype(f32), third.astype(f32)], axis=0)
    summed = dot(pieces.astype(bf16), upto, ((1,), (0,)))
    cumul = summed[0:8] + summed[8:16] + summed[16:24]
    rows_ref[...] = cumul
    cols = cumul.T
    cols_ref[...] = cols
    last = cols[tokens - 1 : tokens, :]
    lead = jnp.exp(cols)
    tail = jnp.exp(last - cols)
    weights_ref[...] = jnp.concatenate([lead, tail], axis=1)
    total = jnp.exp(last)
    x_turned = x_ref[...].T
    g_turned = g_ref[...].T
    write = write_ref[...].astype(f32)
    read = read_ref[...].astype(f32)
    per_head = head_size // chunk
    for head in range(heads):
        own = slice(head * head_size, (head + 1) * head_size)
        state = dot(
            x_turned[own],
            jnp.concatenate(split(write * tail[:, head : head + 1]), axis=1),
            ((1,), (0,)),
        )
        grad = dot(
            g_turned[own],
            jnp.concatenate(split(read * lead[:, head : head + 1]), axis=1),
            ((1,), (0,)),
        )
        width = state.shape[1] // 2
        state = state[:, :width] + state[:, width:]
        grad = grad[:, :width] + grad[:, width:]
        total_row = jnp.broadcast_to(total[:, head : head + 1], (1, width))
        for part in range(per_head):
            base = (head * per_head + part) * (2 * chunk + 1)
            at = slice(part * chunk, (part + 1) * chunk)
            send_ref[base : base + chunk, :] = state[at]
            send_ref[base + chunk : base + 2 * chunk, :] = grad[at]
            send_ref[base + 2 * chunk : base + 2 * chunk + 1, :] = total_row


def scan_kernel(sections, chunk, got_ref, out_ref):
    stride = 2 * chunk + 1

    def total(section):
        base = section * stride + 2 * chunk
        return got_ref[base : base + 1, :]

    running = jnp.zeros((chunk, got_ref.shape[1]), f32)
    for section in range(sections):
        base = section * stride
        out_ref[section, 0:chunk, :] = running
        running = total(section) * running + got_ref[base : base + chunk, :]
    running = jnp.zeros((chunk, got_ref.shape[1]), f32)
    for section in range(sections - 1, -1, -1):
        base = section * stride + chunk
        out_ref[section, chunk : 2 * chunk, :] = running
        running = total(section) * running + got_ref[base : base + chunk, :]


def intra_kernel(
    heads, x_ref, g_ref, write_ref, read_ref, rows_ref, cols_ref, y_ref, dx_ref, grad_ref
):
    tokens, channels = x_ref.shape
    head_size = channels // heads
    width = write_ref.shape[1]
    blocks = tokens // BLOCK
    y_ref[...] = jnp.zeros_like(y_ref)
    dx_ref[...] = jnp.zeros_like(dx_ref)
    grad_ref[...] = jnp.zeros_like(grad_ref)
    causal = lax.broadcasted_iota(jnp.int32, (BLOCK, BLOCK), 0) >= lax.broadcasted_iota(
        jnp.int32, (BLOCK, BLOCK), 1
    )
    for later in range(blocks):
        t = slice(later * BLOCK, (later + 1) * BLOCK)
        read = read_ref[t, :]
        g_block = g_ref[t, :]
        for earlier in range(later + 1):
            j = slice(earlier * BLOCK, (earlier + 1) * BLOCK)
            write = write_ref[j, :]
            x_block = x_ref[j, :]
            scores = dot(read, write, ((1,), (1,)))
            score_grad = jnp.zeros((BLOCK, BLOCK), f32)
            for head in range(heads):
                own = slice(head * head_size, (head + 1) * head_size)
                differ = cols_ref[t, head : head + 1] - rows_ref[head : head + 1, j]
                if later == earlier:
                    differ = jnp.where(causal, differ, -jnp.inf)
                decay = jnp.exp(differ)
                mixing = (scores * decay).astype(bf16)
                x_head = x_block[:, own]
                g_head = g_block[:, own]
                y_ref[t, own] += dot(mixing, x_head, ((1,), (0,)))
                dx_ref[j, own] += dot(mixing, g_head, ((0,), (0,)))
                score_grad += dot(g_head, x_head, ((1,), (1,))) * decay
            high, low = split(score_grad)
            grad_ref[j, 0:width] += dot(high, read, ((0,), (0,))) + dot(low, read, ((0,), (0,)))
            grad_ref[t, width:] += dot(high, write, ((1,), (0,))) + dot(low, write, ((1,), (0,)))


def states_of(state_ref, chunk):
    forward = state_ref[:, 0:chunk, :]
    backward = state_ref[:, chunk:, :]
    flat = (forward.shape[0] * chunk, forward.shape[2])
    return forward.reshape(flat), backward.reshape(flat)


def carried(values, state, columns, heads):
    rows, width = state.shape
    row_head = lax.broadcasted_iota(jnp.int32, (rows, 1), 0) // (rows // heads)
    total = None
    for head in range(heads):
        mine = jnp.where(row_head == head, state, 0.0)
        product = dot(values, jnp.concatenate(split(mine), axis=1), ((1,), (0,)))
        product = (product[:, :width] + product[:, width:]) * columns[:, head : head + 1]
        total = product if total is None else total + product
    return total


def carry_kernel(heads, chunk, group, core_ref, state_ref, x_ref, g_ref, weights_ref, intra_ref, keep_ref, send_ref):
    forward, backward = states_of(state_ref, chunk)
    width = forward.shape[1]
    count = keep_ref.shape[0]
    lead = weights_ref[:, 0:8]
    tail = weights_ref[:, 8:16]
    of_write = carried(x_ref[...], backward, tail, heads) + intra_ref[:, 0:width]
    of_read = carried(g_ref[...], forward, lead, heads) + intra_ref[:, width:]
    whole = jnp.concatenate([of_write, of_read], axis=1).reshape(count, 2, group, 2 * width)

    @pl.when(core_ref[0] == 0)
    def _():
        keep_ref[...] = whole[:, 0]
        send_ref[...] = whole[:, 1]

    @pl.when(core_ref[0] != 0)
    def _():
        keep_ref[...] = whole[:, 1]
        send_ref[...] = whole[:, 0]


def finish_kernel(
    heads, chunk, state_ref, write_ref, read_ref, weights_ref, y_ref, dx_ref, out_ref, dout_ref
):
    forward, backward = states_of(state_ref, chunk)
    head_size = forward.shape[0] // heads
    read, write = read_ref[...], write_ref[...]

    def inter(tokens, state):
        return dot(
            jnp.concatenate([tokens, tokens], axis=1),
            jnp.concatenate(split(state), axis=1),
            ((1,), (1,)),
        )

    lead = lanes_of_heads(weights_ref[:, 0:8], heads, head_size)
    out_ref[...] = (y_ref[...] + inter(read, forward) * lead).astype(bf16)
    tail = lanes_of_heads(weights_ref[:, 8:16], heads, head_size)
    dout_ref[...] = (dx_ref[...] + inter(write, backward) * tail).astype(bf16)


def call(kernel, outs, name, count, cost):
    return pl.pallas_call(
        kernel,
        out_shape=[jax.ShapeDtypeStruct(shape, dtype) for shape, dtype in outs],
        in_specs=[VMEM] * count if isinstance(count, int) else count,
        out_specs=[VMEM] * len(outs),
        compiler_params=pltpu.CompilerParams(vmem_limit_bytes=40 * 2**20),
        cost_estimate=pl.CostEstimate(flops=cost, bytes_accessed=4 * 2**20, transcendentals=0),
        name=name,
    )


def per_device(sections, spread, inputs, log_decay, write_proj, read_proj, grad_out):
    tokens, channels = inputs.shape
    heads = log_decay.shape[0]
    width = write_proj.shape[1]
    chunk = channels // sections
    stride = 2 * chunk + 1
    group = tokens // (2 * spread)
    send, rows, cols, weights = call(
        functools.partial(local_kernel, sections),
        [((sections * stride, width), f32), ((8, tokens), f32), ((tokens, 8), f32), ((tokens, 16), f32)],
        "local",
        5,
        10**9,
    )(inputs, grad_out, write_proj, read_proj, log_decay)
    got = lax.all_to_all(send.reshape(sections, stride, 1, width), ("x", "zh"), 0, 0)
    got = got.reshape(sections * stride, width)
    y_intra, dx_intra, grad_intra = call(
        functools.partial(intra_kernel, heads),
        [((tokens, channels), f32), ((tokens, channels), f32), ((tokens, 2 * width), f32)],
        "intra",
        6,
        8 * 10**9,
    )(inputs, grad_out, write_proj, read_proj, rows, cols)
    (states,) = call(
        functools.partial(scan_kernel, sections, chunk),
        [((sections, 2 * chunk, width), f32)],
        "scan",
        1,
        10**8,
    )(got)
    mine = lax.all_to_all(states, ("x", "zh"), 0, 0)
    core = lax.axis_index("core").reshape(1)
    keep, away = call(
        functools.partial(carry_kernel, heads, chunk, group),
        [((spread, group, 2 * width), f32)] * 2,
        "carry",
        [SMEM] + [VMEM] * 5,
        10**9,
    )(core, mine, inputs, grad_out, weights, grad_intra)
    other = lax.ppermute(away, "core", [(0, 1), (1, 0)])
    parts = lax.all_to_all(keep + other, ("y", "zl"), 0, 0)
    outputs, grad_inputs = call(
        functools.partial(finish_kernel, heads, chunk),
        [((tokens, channels), bf16)] * 2,
        "finish",
        6,
        2 * 10**9,
    )(mine, write_proj, read_proj, weights, y_intra, dx_intra)
    summed = jnp.sum(parts, axis=0)
    return (outputs, grad_inputs, summed[:, :width], summed[:, width:])


def solution(mesh, shape=(8, 4, 8, 2, 2)):
    axes = ("x", "zh", "y", "zl", "core")
    fine = Mesh(mesh.devices.reshape(shape), axes)
    seq, head = axes[:2], axes[2:]
    return jax.shard_map(
        functools.partial(per_device, shape[0] * shape[1], shape[2] * shape[3]),
        mesh=fine,
        in_specs=(P(seq, head), P(head, seq), P(seq, None), P(seq, None), P(seq, head)),
        out_specs=(P(seq, head), P(seq, head), P(axes, None), P(axes, None)),
        check_vma=False,
    )
```

```python
import functools

import jax
import jax.numpy as jnp
from jax import lax
from jax.experimental import pallas as pl
from jax.experimental.pallas import tpu as pltpu
from jax.sharding import Mesh, PartitionSpec as P

f32 = jnp.float32
bf16 = jnp.bfloat16
VMEM = pl.BlockSpec(memory_space=pltpu.VMEM)
SMEM = pl.BlockSpec(memory_space=pltpu.SMEM)
ANY = pl.BlockSpec(memory_space=pl.ANY)
BLOCK = 256


def dot(a, b, dims):
    return lax.dot_general(a, b, (dims, ((), ())), preferred_element_type=f32)


def split(value):
    high = value.astype(bf16)
    return high, (value - high.astype(f32)).astype(bf16)


def lanes_of_heads(columns, heads, width):
    tokens = columns.shape[0]
    lane = lax.broadcasted_iota(jnp.int32, (tokens, heads * width), 1) // width
    spread = jnp.broadcast_to(columns[:, 0:1], (tokens, heads * width))
    for head in range(1, heads):
        spread = jnp.where(lane == head, columns[:, head : head + 1], spread)
    return spread


def local_kernel(
    sections,
    x_hbm,
    g_hbm,
    write_hbm,
    read_hbm,
    decay_hbm,
    send_ref,
    rows_ref,
    cols_ref,
    x_ref,
    g_ref,
    write_ref,
    read_ref,
    decay_ref,
    arrived,
):
    pairs = (
        (decay_hbm, decay_ref),
        (x_hbm, x_ref),
        (write_hbm, write_ref),
        (g_hbm, g_ref),
        (read_hbm, read_ref),
    )
    copies = [
        pltpu.make_async_copy(source, target, arrived.at[at])
        for at, (source, target) in enumerate(pairs)
    ]
    for copy in copies:
        copy.start()
    heads, tokens = decay_ref.shape
    channels = x_ref.shape[1]
    head_size = channels // heads
    chunk = channels // sections
    lanes = 128
    upto = (
        lax.broadcasted_iota(jnp.int32, (lanes, lanes), 0)
        <= lax.broadcasted_iota(jnp.int32, (lanes, lanes), 1)
    ).astype(f32).astype(bf16)
    copies[0].wait()
    decay = jnp.concatenate([decay_ref[...], jnp.zeros((8 - heads, tokens), f32)], axis=0)
    first, _ = split(decay)
    second, third = split(decay - first.astype(f32))
    wide = jnp.concatenate([first.astype(f32), second.astype(f32), third.astype(f32)], axis=0)
    count = tokens // lanes
    stacked = jnp.concatenate(
        [wide[:, part * lanes : (part + 1) * lanes] for part in range(count)], axis=0
    ).astype(bf16)
    summed = dot(stacked, upto, ((1,), (0,)))
    parts = []
    before = jnp.zeros((8, 1), f32)
    for part in range(count):
        base = 24 * part
        inside = summed[base : base + 8] + summed[base + 8 : base + 16] + summed[base + 16 : base + 24]
        parts.append(inside + before)
        before = before + inside[:, lanes - 1 : lanes]
    cumul = jnp.concatenate(parts, axis=1)
    rows_ref[...] = cumul
    total = jnp.exp(before)
    cols = jnp.concatenate([cumul, jnp.exp(cumul), jnp.exp(before - cumul)], axis=0).T
    cols_ref[...] = cols
    per_head = head_size // chunk
    for flow, (values_ref, vectors_ref, column) in enumerate(
        ((x_ref, write_ref, 16), (g_ref, read_ref, 8))
    ):
        copies[1 + 2 * flow].wait()
        turned = values_ref[...].T
        copies[2 + 2 * flow].wait()
        vectors = vectors_ref[...].astype(f32)
        width = vectors.shape[1]
        for head in range(heads):
            state = dot(
                turned[head * head_size : (head + 1) * head_size],
                jnp.concatenate(split(vectors * cols[:, column + head : column + head + 1]), axis=1),
                ((1,), (0,)),
            )
            state = state[:, :width] + state[:, width:]
            for part in range(per_head):
                base = (head * per_head + part) * (2 * chunk + 1)
                at = base + flow * chunk
                send_ref[at : at + chunk, :] = state[part * chunk : (part + 1) * chunk]
                if flow == 0:
                    at = base + 2 * chunk
                    send_ref[at : at + 1, :] = jnp.broadcast_to(total[head : head + 1], (1, width))


def scan_kernel(sections, chunk, got_ref, cross_ref, out_ref, crossed_ref):
    stride = 2 * chunk + 1

    def total(section):
        base = section * stride + 2 * chunk
        return got_ref[base : base + 1, :]

    running = jnp.zeros((chunk, got_ref.shape[1]), f32)
    for section in range(sections):
        base = section * stride
        out_ref[section, 1] = running
        running = total(section) * running + got_ref[base : base + chunk, :]
    running = jnp.zeros((chunk, got_ref.shape[1]), f32)
    for section in range(sections - 1, -1, -1):
        base = section * stride + chunk
        out_ref[section, 0] = running
        running = total(section) * running + got_ref[base : base + chunk, :]


def intra_kernel(
    heads,
    core_ref,
    x_ref,
    g_ref,
    write_ref,
    read_ref,
    rows_ref,
    cols_ref,
    y_ref,
    dx_ref,
    own_ref,
    cross_ref,
    grad_ref,
):
    tokens, channels = x_ref.shape
    head_size = channels // heads
    width = write_ref.shape[1]
    blocks = tokens // BLOCK
    y_ref[...] = jnp.zeros_like(y_ref)
    dx_ref[...] = jnp.zeros_like(dx_ref)
    grad_ref[...] = jnp.zeros_like(grad_ref)
    causal = lax.broadcasted_iota(jnp.int32, (BLOCK, BLOCK), 0) >= lax.broadcasted_iota(
        jnp.int32, (BLOCK, BLOCK), 1
    )
    for later in range(blocks):
        t = slice(later * BLOCK, (later + 1) * BLOCK)
        read = read_ref[t, :]
        g_block = g_ref[t, :]
        for earlier in range(later + 1):
            j = slice(earlier * BLOCK, (earlier + 1) * BLOCK)
            write = write_ref[j, :]
            x_block = x_ref[j, :]
            scores = dot(read, write, ((1,), (1,)))
            score_grad = jnp.zeros((BLOCK, BLOCK), f32)
            for head in range(heads):
                own = slice(head * head_size, (head + 1) * head_size)
                differ = cols_ref[t, head : head + 1] - rows_ref[head : head + 1, j]
                if later == earlier:
                    differ = jnp.where(causal, differ, -jnp.inf)
                decay = jnp.exp(differ)
                mixing = (scores * decay).astype(bf16)
                x_head = x_block[:, own]
                g_head = g_block[:, own]
                y_ref[t, own] += dot(mixing, x_head, ((1,), (0,)))
                dx_ref[j, own] += dot(mixing, g_head, ((0,), (0,)))
                score_grad += dot(g_head, x_head, ((1,), (1,))) * decay
            high, low = split(score_grad)
            grad_ref[j, 0:width] += dot(high, read, ((0,), (0,))) + dot(low, read, ((0,), (0,)))
            grad_ref[t, width:] += dot(high, write, ((1,), (0,))) + dot(low, write, ((1,), (0,)))
    first = core_ref[0] == 0
    own_ref[:, channels:] = jnp.where(first, grad_ref[:, 0:width], grad_ref[:, width:])
    cross_ref[:, channels:] = jnp.where(first, grad_ref[:, width:], grad_ref[:, 0:width])
    x_weighted = x_ref[...].astype(f32) * lanes_of_heads(cols_ref[:, 16:24], heads, head_size)
    g_weighted = g_ref[...].astype(f32) * lanes_of_heads(cols_ref[:, 8:16], heads, head_size)
    own_ref[:, 0:channels] = jnp.where(first, x_weighted, g_weighted)
    cross_ref[:, 0:channels] = jnp.where(first, g_weighted, x_weighted)


def carry_kernel(core_ref, state_ref, own_ref, other_ref, out_ref, kept_ref, swap_ref):
    core = core_ref[0]
    channels = own_ref.shape[1] - out_ref.shape[1]
    width = out_ref.shape[1]
    flat = (channels, width)
    mine = state_ref[:, pl.ds(core, 1)].reshape(flat)
    partner = state_ref[:, pl.ds(1 - core, 1)].reshape(flat)
    kept_ref[...] = mine
    swap_ref[...] = partner
    total = own_ref[:, channels:] + other_ref[:, channels:]
    for values_ref, state in ((own_ref, mine), (other_ref, partner)):
        high, low = split(values_ref[:, 0:channels])
        state_high, state_low = split(state)
        product = dot(high, jnp.concatenate([state_high, state_low], axis=1), ((1,), (0,)))
        total += product[:, :width] + product[:, width:] + dot(low, state_high, ((1,), (0,)))
    out_ref[...] = total


def finish_kernel(
    heads, core_ref, kept_ref, came_ref, write_ref, read_ref, cols_ref, y_ref, dx_ref, out_ref, dout_ref
):
    first = core_ref[0] == 0
    forward = jnp.where(first, came_ref[...], kept_ref[...])
    backward = jnp.where(first, kept_ref[...], came_ref[...])
    head_size = forward.shape[0] // heads
    read, write = read_ref[...], write_ref[...]

    def inter(tokens, state):
        return dot(
            jnp.concatenate([tokens, tokens], axis=1),
            jnp.concatenate(split(state), axis=1),
            ((1,), (1,)),
        )

    lead = lanes_of_heads(cols_ref[:, 8:16], heads, head_size)
    out_ref[...] = (y_ref[...] + inter(read, forward) * lead).astype(bf16)
    tail = lanes_of_heads(cols_ref[:, 16:24], heads, head_size)
    dout_ref[...] = (dx_ref[...] + inter(write, backward) * tail).astype(bf16)


def call(kernel, outs, specs, cost, mebibytes, scratch=(), out_specs=None, **more):
    return pl.pallas_call(
        kernel,
        out_shape=[jax.ShapeDtypeStruct(shape, dtype) for shape, dtype in outs],
        in_specs=specs,
        out_specs=out_specs or [VMEM] * len(outs),
        scratch_shapes=list(scratch),
        compiler_params=pltpu.CompilerParams(vmem_limit_bytes=mebibytes * 2**20),
        cost_estimate=pl.CostEstimate(flops=cost, bytes_accessed=4 * 2**20, transcendentals=0),
        **more,
    )


def per_device(sections, spread, inputs, log_decay, write_proj, read_proj, grad_out):
    tokens, channels = inputs.shape
    heads = log_decay.shape[0]
    width = write_proj.shape[1]
    chunk = channels // sections
    stride = 2 * chunk + 1
    core = lax.axis_index("core").reshape(1)
    swap_cores = [(0, 1), (1, 0)]
    send, rows, cols = call(
        functools.partial(local_kernel, sections),
        [((sections * stride, width), f32), ((8, tokens), f32), ((tokens, 24), f32)],
        [ANY] * 5,
        10**9,
        60,
        [
            pltpu.VMEM(inputs.shape, bf16),
            pltpu.VMEM(inputs.shape, bf16),
            pltpu.VMEM(write_proj.shape, bf16),
            pltpu.VMEM(write_proj.shape, bf16),
            pltpu.VMEM(log_decay.shape, f32),
            pltpu.SemaphoreType.DMA((5,)),
        ],
    )(inputs, grad_out, write_proj, read_proj, log_decay)
    got = lax.all_to_all(send.reshape(sections, stride, 1, width), ("x", "zh"), 0, 0)
    got = got.reshape(sections * stride, width)
    y_intra, dx_intra, own, cross = call(
        functools.partial(intra_kernel, heads),
        [
            ((tokens, channels), f32),
            ((tokens, channels), f32),
            ((tokens, channels + width), f32),
            ((tokens, channels + width), f32),
        ],
        [SMEM] + [VMEM] * 6,
        8 * 10**9,
        16,
        [pltpu.VMEM((tokens, 2 * width), f32)],
    )(core, inputs, grad_out, write_proj, read_proj, rows, cols)
    states, cross = call(
        functools.partial(scan_kernel, sections, chunk),
        [((sections, 2, chunk, width), f32), (cross.shape, f32)],
        [VMEM, ANY],
        10**8,
        4,
        out_specs=[VMEM, ANY],
        input_output_aliases={1: 1},
    )(got, cross)
    mine = lax.all_to_all(
        states.reshape(2 * sections, chunk, width), ("x", "zh", "core"), 0, 0
    ).reshape(sections, 2, chunk, width)
    other = lax.ppermute(cross, "core", swap_cores)
    piece, kept, swap = call(
        carry_kernel,
        [((tokens, width), f32), ((channels, width), f32), ((channels, width), f32)],
        [SMEM] + [VMEM] * 3,
        10**9,
        12,
    )(core, mine, own, other)
    parts = lax.all_to_all(
        piece.reshape(2 * spread, tokens // (2 * spread), width), ("y", "zl", "core"), 0, 0
    )
    came = lax.ppermute(swap, "core", swap_cores)
    outputs, grad_inputs = call(
        functools.partial(finish_kernel, heads),
        [((tokens, channels), bf16)] * 2,
        [SMEM] + [VMEM] * 7,
        2 * 10**9,
        12,
    )(core, kept, came, write_proj, read_proj, cols, y_intra, dx_intra)
    summed = jnp.sum(parts.reshape(spread, 2, -1, width), axis=0)
    return (outputs, grad_inputs, summed[0], summed[1])


def solution(mesh, shape=(8, 4, 8, 2, 2)):
    axes = ("x", "zh", "y", "zl", "core")
    fine = Mesh(mesh.devices.reshape(shape), axes)
    seq, head = axes[:2], axes[2:]
    return jax.shard_map(
        functools.partial(per_device, shape[0] * shape[1], shape[2] * shape[3]),
        mesh=fine,
        in_specs=(P(seq, head), P(head, seq), P(seq, None), P(seq, None), P(seq, head)),
        out_specs=(P(seq, head), P(seq, head), P(axes, None), P(axes, None)),
        check_vma=False,
    )
```

```python
import functools

import jax
import jax.numpy as jnp
from jax import lax
from jax.experimental import pallas as pl
from jax.experimental.pallas import tpu as pltpu
from jax.sharding import Mesh, PartitionSpec as P

f32 = jnp.float32
bf16 = jnp.bfloat16
VMEM = pl.BlockSpec(memory_space=pltpu.VMEM)
SMEM = pl.BlockSpec(memory_space=pltpu.SMEM)
ANY = pl.BlockSpec(memory_space=pl.ANY)
BLOCK = 256


def dot(a, b, dims):
    return lax.dot_general(a, b, (dims, ((), ())), preferred_element_type=f32)


def split(value):
    high = value.astype(bf16)
    return high, (value - high.astype(f32)).astype(bf16)


def lanes_of_heads(columns, heads, width):
    tokens = columns.shape[0]
    lane = lax.broadcasted_iota(jnp.int32, (tokens, heads * width), 1) // width
    spread = jnp.broadcast_to(columns[:, 0:1], (tokens, heads * width))
    for head in range(1, heads):
        spread = jnp.where(lane == head, columns[:, head : head + 1], spread)
    return spread


def local_kernel(
    sections,
    x_hbm,
    g_hbm,
    write_hbm,
    read_hbm,
    decay_hbm,
    send_ref,
    rows_ref,
    x_ref,
    g_ref,
    write_ref,
    read_ref,
    decay_ref,
    arrived,
):
    pairs = (
        (decay_hbm, decay_ref),
        (x_hbm, x_ref),
        (write_hbm, write_ref),
        (g_hbm, g_ref),
        (read_hbm, read_ref),
    )
    copies = [
        pltpu.make_async_copy(source, target, arrived.at[at])
        for at, (source, target) in enumerate(pairs)
    ]
    for copy in copies:
        copy.start()
    heads, tokens = decay_ref.shape
    channels = x_ref.shape[1]
    head_size = channels // heads
    chunk = channels // sections
    lanes = 128
    upto = (
        lax.broadcasted_iota(jnp.int32, (lanes, lanes), 0)
        <= lax.broadcasted_iota(jnp.int32, (lanes, lanes), 1)
    ).astype(f32).astype(bf16)
    copies[0].wait()
    decay = jnp.concatenate([decay_ref[...], jnp.zeros((8 - heads, tokens), f32)], axis=0)
    first, _ = split(decay)
    second, third = split(decay - first.astype(f32))
    wide = jnp.concatenate([first.astype(f32), second.astype(f32), third.astype(f32)], axis=0)
    count = tokens // lanes
    stacked = jnp.concatenate(
        [wide[:, part * lanes : (part + 1) * lanes] for part in range(count)], axis=0
    ).astype(bf16)
    summed = dot(stacked, upto, ((1,), (0,)))
    parts = []
    before = jnp.zeros((8, 1), f32)
    for part in range(count):
        base = 24 * part
        inside = summed[base : base + 8] + summed[base + 8 : base + 16] + summed[base + 16 : base + 24]
        parts.append(inside + before)
        before = before + inside[:, lanes - 1 : lanes]
    cumul = jnp.concatenate(parts, axis=1)
    rows = jnp.concatenate([cumul, jnp.exp(cumul), jnp.exp(before - cumul)], axis=0)
    rows_ref[...] = rows
    total = jnp.exp(before)
    cols = rows.T
    per_head = head_size // chunk
    for flow, (values_ref, vectors_ref, column) in enumerate(
        ((x_ref, write_ref, 16), (g_ref, read_ref, 8))
    ):
        copies[1 + 2 * flow].wait()
        turned = values_ref[...].T
        copies[2 + 2 * flow].wait()
        vectors = vectors_ref[...].astype(f32)
        width = vectors.shape[1]
        for head in range(heads):
            state = dot(
                turned[head * head_size : (head + 1) * head_size],
                jnp.concatenate(split(vectors * cols[:, column + head : column + head + 1]), axis=1),
                ((1,), (0,)),
            )
            state = state[:, :width] + state[:, width:]
            for part in range(per_head):
                base = (head * per_head + part) * (2 * chunk + 1)
                at = base + flow * chunk
                send_ref[at : at + chunk, :] = state[part * chunk : (part + 1) * chunk]
                if flow == 0:
                    at = base + 2 * chunk
                    send_ref[at : at + 1, :] = jnp.broadcast_to(total[head : head + 1], (1, width))


def scan_kernel(sections, chunk, got_ref, after_ref, out_ref):
    stride = 2 * chunk + 1

    def total(section):
        base = section * stride + 2 * chunk
        return got_ref[base : base + 1, :]

    running = jnp.zeros((chunk, got_ref.shape[1]), f32)
    for section in range(sections):
        base = section * stride
        out_ref[section, 1] = running
        running = total(section) * running + got_ref[base : base + chunk, :]
    running = jnp.zeros((chunk, got_ref.shape[1]), f32)
    for section in range(sections - 1, -1, -1):
        base = section * stride + chunk
        out_ref[section, 0] = running
        running = total(section) * running + got_ref[base : base + chunk, :]


def intra_kernel(
    heads,
    core_ref,
    x_ref,
    g_ref,
    write_ref,
    read_ref,
    rows_ref,
    y_hbm,
    dx_hbm,
    own_hbm,
    cross_hbm,
    after_ref,
    y_ref,
    dx_ref,
    own_ref,
    cross_ref,
    grad_ref,
    left,
):
    tokens, channels = x_ref.shape
    head_size = channels // heads
    width = write_ref.shape[1]
    blocks = tokens // BLOCK
    after_ref[0] = 0
    started = []

    def leave(source, target):
        copy = pltpu.make_async_copy(source, target, left.at[len(started)])
        copy.start()
        started.append(copy)

    first = core_ref[0] == 0
    cols = rows_ref[...].T
    x_weighted = x_ref[...].astype(f32) * lanes_of_heads(cols[:, 16:24], heads, head_size)
    g_weighted = g_ref[...].astype(f32) * lanes_of_heads(cols[:, 8:16], heads, head_size)
    own_ref[:, 0:channels] = jnp.where(first, x_weighted, g_weighted)
    cross_ref[:, 0:channels] = jnp.where(first, g_weighted, x_weighted)
    for source, target in ((own_ref, own_hbm), (cross_ref, cross_hbm)):
        leave(source.at[:, pl.ds(0, channels)], target.at[:, pl.ds(0, channels)])
    y_ref[...] = jnp.zeros_like(y_ref)
    dx_ref[...] = jnp.zeros_like(dx_ref)
    grad_ref[...] = jnp.zeros_like(grad_ref)
    causal = lax.broadcasted_iota(jnp.int32, (BLOCK, BLOCK), 0) >= lax.broadcasted_iota(
        jnp.int32, (BLOCK, BLOCK), 1
    )
    for later in range(blocks):
        t = slice(later * BLOCK, (later + 1) * BLOCK)
        read = read_ref[t, :]
        g_block = g_ref[t, :]
        for earlier in range(later + 1):
            j = slice(earlier * BLOCK, (earlier + 1) * BLOCK)
            write = write_ref[j, :]
            x_block = x_ref[j, :]
            scores = dot(read, write, ((1,), (1,)))
            score_grad = jnp.zeros((BLOCK, BLOCK), f32)
            for head in range(heads):
                own = slice(head * head_size, (head + 1) * head_size)
                differ = cols[t, head : head + 1] - rows_ref[head : head + 1, j]
                if later == earlier:
                    differ = jnp.where(causal, differ, -jnp.inf)
                decay = jnp.exp(differ)
                mixing = (scores * decay).astype(bf16)
                x_head = x_block[:, own]
                g_head = g_block[:, own]
                y_ref[t, own] += dot(mixing, x_head, ((1,), (0,)))
                dx_ref[j, own] += dot(mixing, g_head, ((0,), (0,)))
                score_grad += dot(g_head, x_head, ((1,), (1,))) * decay
            if later == blocks - 1:
                at = pl.ds(earlier * BLOCK, BLOCK)
                leave(dx_ref.at[at], dx_hbm.at[at])
            high, low = split(score_grad)
            grad_ref[j, 0:width] += dot(high, read, ((0,), (0,))) + dot(low, read, ((0,), (0,)))
            grad_ref[t, width:] += dot(high, write, ((1,), (0,))) + dot(low, write, ((1,), (0,)))
        at = pl.ds(later * BLOCK, BLOCK)
        leave(y_ref.at[at], y_hbm.at[at])
    own_ref[:, channels:] = jnp.where(first, grad_ref[:, 0:width], grad_ref[:, width:])
    cross_ref[:, channels:] = jnp.where(first, grad_ref[:, width:], grad_ref[:, 0:width])
    for source, target in ((own_ref, own_hbm), (cross_ref, cross_hbm)):
        leave(source.at[:, pl.ds(channels, width)], target.at[:, pl.ds(channels, width)])
    for copy in started:
        copy.wait()


def carry_kernel(
    core_ref, state_ref, came_ref, own_hbm, other_hbm, out_ref, own_ref, other_ref, arrived
):
    blocks = own_ref.shape[0] // BLOCK
    copies = []
    for block in range(blocks):
        at = pl.ds(block * BLOCK, BLOCK)
        for flow, (source, target) in enumerate(((own_hbm, own_ref), (other_hbm, other_ref))):
            copy = pltpu.make_async_copy(source.at[at], target.at[at], arrived.at[block, flow])
            copy.start()
            copies.append(copy)
    core = core_ref[0]
    width = out_ref.shape[1]
    channels = own_ref.shape[1] - width
    factors = []
    for states_ref in (state_ref, came_ref):
        high, low = split(states_ref[:, pl.ds(core, 1)].reshape(channels, width))
        factors.append((jnp.concatenate([high, low], axis=1), high))
    for block in range(blocks):
        t = slice(block * BLOCK, (block + 1) * BLOCK)
        copies[2 * block].wait()
        copies[2 * block + 1].wait()
        total = own_ref[t, channels:] + other_ref[t, channels:]
        for values_ref, (both, first) in zip((own_ref, other_ref), factors):
            high, low = split(values_ref[t, 0:channels])
            product = dot(high, both, ((1,), (0,)))
            total += product[:, :width] + product[:, width:] + dot(low, first, ((1,), (0,)))
        out_ref[t, :] = total


def finish_kernel(
    heads, state_ref, write_ref, read_ref, rows_ref, y_ref, dx_ref, out_ref, dout_ref
):
    channels, width = out_ref.shape[1], write_ref.shape[1]
    backward = state_ref[:, 0].reshape(channels, width)
    forward = state_ref[:, 1].reshape(channels, width)
    head_size = forward.shape[0] // heads
    read, write = read_ref[...], write_ref[...]

    def inter(tokens, state):
        return dot(
            jnp.concatenate([tokens, tokens], axis=1),
            jnp.concatenate(split(state), axis=1),
            ((1,), (1,)),
        )

    cols = rows_ref[...].T
    lead = lanes_of_heads(cols[:, 8:16], heads, head_size)
    out_ref[...] = (y_ref[...] + inter(read, forward) * lead).astype(bf16)
    tail = lanes_of_heads(cols[:, 16:24], heads, head_size)
    dout_ref[...] = (dx_ref[...] + inter(write, backward) * tail).astype(bf16)


def in_hbm(value):
    return pltpu.with_memory_space_constraint(value, pltpu.HBM)


def call(kernel, outs, specs, cost, mebibytes, out_specs=None, **more):
    return pl.pallas_call(
        kernel,
        out_shape=[jax.ShapeDtypeStruct(shape, dtype) for shape, dtype in outs],
        in_specs=specs,
        out_specs=out_specs or [VMEM] * len(outs),
        compiler_params=pltpu.CompilerParams(vmem_limit_bytes=int(mebibytes * 2**20)),
        cost_estimate=pl.CostEstimate(flops=cost, bytes_accessed=4 * 2**20, transcendentals=0),
        **more,
    )


def per_device(sections, spread, inputs, log_decay, write_proj, read_proj, grad_out):
    tokens, channels = inputs.shape
    heads = log_decay.shape[0]
    width = write_proj.shape[1]
    chunk = channels // sections
    stride = 2 * chunk + 1
    core = lax.axis_index("core").reshape(1)
    swap_cores = [(0, 1), (1, 0)]
    wide = channels + width
    send, rows = call(
        functools.partial(local_kernel, sections),
        [((sections * stride, width), f32), ((24, tokens), f32)],
        [ANY] * 5,
        10**9,
        16,
        scratch_shapes=[
            pltpu.VMEM(inputs.shape, bf16),
            pltpu.VMEM(inputs.shape, bf16),
            pltpu.VMEM(write_proj.shape, bf16),
            pltpu.VMEM(write_proj.shape, bf16),
            pltpu.VMEM(log_decay.shape, f32),
            pltpu.SemaphoreType.DMA((5,)),
        ],
    )(*(in_hbm(value) for value in (inputs, grad_out, write_proj, read_proj, log_decay)))
    got = lax.all_to_all(send.reshape(sections, stride, 1, width), ("x", "zh"), 0, 0)
    got = got.reshape(sections * stride, width)
    y_intra, dx_intra, own, cross, after = call(
        functools.partial(intra_kernel, heads),
        [
            ((tokens, channels), f32),
            ((tokens, channels), f32),
            ((tokens, wide), f32),
            ((tokens, wide), f32),
            ((1,), jnp.int32),
        ],
        [SMEM] + [VMEM] * 5,
        8 * 10**9,
        52.0,
        out_specs=[ANY] * 4 + [SMEM],
        scratch_shapes=[
            pltpu.VMEM((tokens, channels), f32),
            pltpu.VMEM((tokens, channels), f32),
            pltpu.VMEM((tokens, wide), f32),
            pltpu.VMEM((tokens, wide), f32),
            pltpu.VMEM((tokens, 2 * width), f32),
            pltpu.SemaphoreType.DMA((2 * (tokens // BLOCK) + 4,)),
        ],
    )(core, inputs, grad_out, write_proj, read_proj, rows)
    (states,) = call(
        functools.partial(scan_kernel, sections, chunk),
        [((sections, 2, chunk, width), f32)],
        [VMEM, SMEM],
        10**8,
        4.0,
    )(got, after)
    mine = lax.all_to_all(states, ("x", "zh"), 0, 0)
    other = lax.ppermute(cross, "core", swap_cores)
    came = lax.ppermute(mine, "core", swap_cores)
    (piece,) = call(
        carry_kernel,
        [((tokens, width), f32)],
        [SMEM, VMEM, VMEM, ANY, ANY],
        10**9,
        16.0,
        scratch_shapes=[
            pltpu.VMEM((tokens, wide), f32),
            pltpu.VMEM((tokens, wide), f32),
            pltpu.SemaphoreType.DMA((tokens // BLOCK, 2)),
        ],
    )(core, mine, came, in_hbm(own), other)
    parts = lax.all_to_all(
        piece.reshape(2 * spread, tokens // (2 * spread), width), ("y", "zl", "core"), 0, 0
    )
    outputs, grad_inputs = call(
        functools.partial(finish_kernel, heads),
        [((tokens, channels), bf16)] * 2,
        [VMEM] * 6,
        2 * 10**9,
        12.0,
    )(mine, write_proj, read_proj, rows, y_intra, dx_intra)
    summed = jnp.sum(parts.reshape(spread, 2, -1, width), axis=0)
    return (outputs, grad_inputs, summed[0], summed[1])


def solution(mesh, shape=(8, 4, 8, 2, 2)):
    axes = ("x", "zh", "y", "zl", "core")
    fine = Mesh(mesh.devices.reshape(shape), axes)
    seq, head = axes[:2], axes[2:]
    return jax.shard_map(
        functools.partial(per_device, shape[0] * shape[1], shape[2] * shape[3]),
        mesh=fine,
        in_specs=(P(seq, head), P(head, seq), P(seq, None), P(seq, None), P(seq, head)),
        out_specs=(P(seq, head), P(seq, head), P(axes, None), P(axes, None)),
        check_vma=False,
    )
```

```python
import functools

import jax
import jax.numpy as jnp
from jax import lax
from jax.experimental import pallas as pl
from jax.experimental.pallas import tpu as pltpu
from jax.sharding import Mesh, PartitionSpec as P

f32 = jnp.float32
bf16 = jnp.bfloat16
VMEM = pl.BlockSpec(memory_space=pltpu.VMEM)
SMEM = pl.BlockSpec(memory_space=pltpu.SMEM)
ANY = pl.BlockSpec(memory_space=pl.ANY)
BLOCK = 256


def dot(a, b, dims):
    return lax.dot_general(a, b, (dims, ((), ())), preferred_element_type=f32)


def split(value):
    high = value.astype(bf16)
    return high, (value - high.astype(f32)).astype(bf16)


def lanes_of_heads(columns, heads, width):
    tokens = columns.shape[0]
    lane = lax.broadcasted_iota(jnp.int32, (tokens, heads * width), 1) // width
    spread = jnp.broadcast_to(columns[:, 0:1], (tokens, heads * width))
    for head in range(1, heads):
        spread = jnp.where(lane == head, columns[:, head : head + 1], spread)
    return spread


def local_kernel(
    sections,
    x_hbm,
    g_hbm,
    write_hbm,
    read_hbm,
    decay_hbm,
    send_ref,
    rows_ref,
    x_ref,
    g_ref,
    write_ref,
    read_ref,
    decay_ref,
    arrived,
):
    pairs = (
        (decay_hbm, decay_ref),
        (x_hbm, x_ref),
        (write_hbm, write_ref),
        (g_hbm, g_ref),
        (read_hbm, read_ref),
    )
    copies = [
        pltpu.make_async_copy(source, target, arrived.at[at])
        for at, (source, target) in enumerate(pairs)
    ]
    for copy in copies:
        copy.start()
    heads, tokens = decay_ref.shape
    channels = x_ref.shape[1]
    head_size = channels // heads
    chunk = channels // sections
    lanes = 128
    upto = (
        lax.broadcasted_iota(jnp.int32, (lanes, lanes), 0)
        <= lax.broadcasted_iota(jnp.int32, (lanes, lanes), 1)
    ).astype(f32).astype(bf16)
    copies[0].wait()
    decay = jnp.concatenate([decay_ref[...], jnp.zeros((8 - heads, tokens), f32)], axis=0)
    first, _ = split(decay)
    second, third = split(decay - first.astype(f32))
    wide = jnp.concatenate([first.astype(f32), second.astype(f32), third.astype(f32)], axis=0)
    count = tokens // lanes
    stacked = jnp.concatenate(
        [wide[:, part * lanes : (part + 1) * lanes] for part in range(count)], axis=0
    ).astype(bf16)
    summed = dot(stacked, upto, ((1,), (0,)))
    parts = []
    before = jnp.zeros((8, 1), f32)
    for part in range(count):
        base = 24 * part
        inside = summed[base : base + 8] + summed[base + 8 : base + 16] + summed[base + 16 : base + 24]
        parts.append(inside + before)
        before = before + inside[:, lanes - 1 : lanes]
    cumul = jnp.concatenate(parts, axis=1)
    rows = jnp.concatenate([cumul, jnp.exp(cumul), jnp.exp(before - cumul)], axis=0)
    rows_ref[...] = rows
    total = jnp.exp(before)
    cols = rows.T
    per_head = head_size // chunk
    for flow, (values_ref, vectors_ref, column) in enumerate(
        ((x_ref, write_ref, 16), (g_ref, read_ref, 8))
    ):
        copies[1 + 2 * flow].wait()
        turned = values_ref[...].T
        copies[2 + 2 * flow].wait()
        vectors = vectors_ref[...].astype(f32)
        width = vectors.shape[1]
        for head in range(heads):
            state = dot(
                turned[head * head_size : (head + 1) * head_size],
                jnp.concatenate(split(vectors * cols[:, column + head : column + head + 1]), axis=1),
                ((1,), (0,)),
            )
            state = state[:, :width] + state[:, width:]
            for part in range(per_head):
                base = (head * per_head + part) * (2 * chunk + 1)
                at = base + flow * chunk
                send_ref[at : at + chunk, :] = state[part * chunk : (part + 1) * chunk]
                if flow == 0:
                    at = base + 2 * chunk
                    send_ref[at : at + 1, :] = jnp.broadcast_to(total[head : head + 1], (1, width))


def scan_kernel(sections, chunk, got_ref, out_ref):
    stride = 2 * chunk + 1

    def total(section):
        base = section * stride + 2 * chunk
        return got_ref[base : base + 1, :]

    running = jnp.zeros((chunk, got_ref.shape[1]), f32)
    for section in range(sections):
        base = section * stride
        out_ref[section, 0:chunk, :] = running
        running = total(section) * running + got_ref[base : base + chunk, :]
    running = jnp.zeros((chunk, got_ref.shape[1]), f32)
    for section in range(sections - 1, -1, -1):
        base = section * stride + chunk
        out_ref[section, chunk : 2 * chunk, :] = running
        running = total(section) * running + got_ref[base : base + chunk, :]


def intra_kernel(
    heads,
    laters,
    x_ref,
    g_ref,
    write_ref,
    read_ref,
    rows_ref,
    y_hbm,
    dx_hbm,
    grad_hbm,
    y_ref,
    dx_ref,
    grad_ref,
    left,
):
    channels = x_ref.shape[1]
    head_size = channels // heads
    width = write_ref.shape[1]
    started = []

    def leave(source, target, first, count):
        at = pl.ds(first, count)
        copy = pltpu.make_async_copy(source.at[at], target.at[at], left.at[len(started)])
        copy.start()
        started.append(copy)

    cols = rows_ref[...].T
    y_ref[...] = jnp.zeros_like(y_ref)
    dx_ref[...] = jnp.zeros_like(dx_ref)
    grad_ref[...] = jnp.zeros_like(grad_ref)
    causal = lax.broadcasted_iota(jnp.int32, (BLOCK, BLOCK), 0) >= lax.broadcasted_iota(
        jnp.int32, (BLOCK, BLOCK), 1
    )
    for place, later in enumerate(laters):
        t = slice(later * BLOCK, (later + 1) * BLOCK)
        mine = slice(place * BLOCK, (place + 1) * BLOCK)
        read = read_ref[t, :]
        g_block = g_ref[t, :]
        for earlier in range(later + 1):
            j = slice(earlier * BLOCK, (earlier + 1) * BLOCK)
            write = write_ref[j, :]
            x_block = x_ref[j, :]
            scores = dot(read, write, ((1,), (1,)))
            score_grad = jnp.zeros((BLOCK, BLOCK), f32)
            for head in range(heads):
                own = slice(head * head_size, (head + 1) * head_size)
                differ = cols[t, head : head + 1] - rows_ref[head : head + 1, j]
                if later == earlier:
                    differ = jnp.where(causal, differ, -jnp.inf)
                decay = jnp.exp(differ)
                mixing = (scores * decay).astype(bf16)
                x_head = x_block[:, own]
                g_head = g_block[:, own]
                y_ref[mine, own] += dot(mixing, x_head, ((1,), (0,)))
                dx_ref[j, own] += dot(mixing, g_head, ((0,), (0,)))
                score_grad += dot(g_head, x_head, ((1,), (1,))) * decay
            high, low = split(score_grad)
            grad_ref[j, 0:width] += dot(high, read, ((0,), (0,))) + dot(low, read, ((0,), (0,)))
            grad_ref[t, width:] += dot(high, write, ((1,), (0,))) + dot(low, write, ((1,), (0,)))
            if place == len(laters) - 1:
                leave(dx_ref, dx_hbm, earlier * BLOCK, BLOCK)
                if earlier < later:
                    leave(grad_ref, grad_hbm, earlier * BLOCK, BLOCK)
        leave(y_ref, y_hbm, place * BLOCK, BLOCK)
    leave(grad_ref, grad_hbm, laters[-1] * BLOCK, BLOCK)
    for copy in started:
        copy.wait()


def states_of(state_ref, chunk):
    forward = state_ref[:, 0:chunk, :]
    backward = state_ref[:, chunk:, :]
    flat = (forward.shape[0] * chunk, forward.shape[2])
    return forward.reshape(flat), backward.reshape(flat)


def carried(values, state, columns, heads):
    rows, width = state.shape
    row_head = lax.broadcasted_iota(jnp.int32, (rows, 1), 0) // (rows // heads)
    total = None
    for head in range(heads):
        mine = jnp.where(row_head == head, state, 0.0)
        product = dot(values, jnp.concatenate(split(mine), axis=1), ((1,), (0,)))
        product = (product[:, :width] + product[:, width:]) * columns[:, head : head + 1]
        total = product if total is None else total + product
    return total


def carry_kernel(
    heads,
    chunk,
    group,
    core_ref,
    state_ref,
    x_ref,
    g_ref,
    rows_ref,
    late_hbm,
    early_hbm,
    keep_ref,
    send_ref,
    late_ref,
    early_ref,
    arrived,
):
    copies = [
        pltpu.make_async_copy(late_hbm, late_ref, arrived.at[0]),
        pltpu.make_async_copy(early_hbm, early_ref, arrived.at[1]),
    ]
    for copy in copies:
        copy.start()
    forward, backward = states_of(state_ref, chunk)
    width = forward.shape[1]
    count = keep_ref.shape[0]
    cols = rows_ref[...].T
    of_write = carried(x_ref[...], backward, cols[:, 16:24], heads)
    of_read = carried(g_ref[...], forward, cols[:, 8:16], heads)
    for copy in copies:
        copy.wait()
    known = early_ref.shape[0]
    late = late_ref[...]
    intra = jnp.concatenate([late[:known] + early_ref[...], late[known:]], axis=0)
    whole = jnp.concatenate([of_write, of_read], axis=1) + intra
    whole = whole.reshape(count, 2, group, 2 * width)

    @pl.when(core_ref[0] == 0)
    def _():
        keep_ref[...] = whole[:, 0]
        send_ref[...] = whole[:, 1]

    @pl.when(core_ref[0] != 0)
    def _():
        keep_ref[...] = whole[:, 1]
        send_ref[...] = whole[:, 0]


def finish_kernel(
    heads,
    chunk,
    state_ref,
    write_ref,
    read_ref,
    rows_ref,
    y_late_ref,
    y_early_ref,
    dx_late_ref,
    dx_early_ref,
    out_ref,
    dout_ref,
):
    forward, backward = states_of(state_ref, chunk)
    head_size = forward.shape[0] // heads
    read, write = read_ref[...], write_ref[...]

    def inter(tokens, state):
        return dot(
            jnp.concatenate([tokens, tokens], axis=1),
            jnp.concatenate(split(state), axis=1),
            ((1,), (1,)),
        )

    known = y_early_ref.shape[0]
    cols = rows_ref[...].T
    outer = inter(read, forward) * lanes_of_heads(cols[:, 8:16], heads, head_size)
    out_ref[0:known, :] = (y_early_ref[...] + outer[:known]).astype(bf16)
    out_ref[known:, :] = (y_late_ref[...] + outer[known:]).astype(bf16)
    outer = inter(write, backward) * lanes_of_heads(cols[:, 16:24], heads, head_size)
    dout_ref[0:known, :] = (dx_late_ref[0:known, :] + dx_early_ref[...] + outer[:known]).astype(bf16)
    dout_ref[known:, :] = (dx_late_ref[known:, :] + outer[known:]).astype(bf16)


def in_hbm(value):
    return pltpu.with_memory_space_constraint(value, pltpu.HBM)


def call(kernel, outs, specs, cost, mebibytes, out_specs=None, **more):
    return pl.pallas_call(
        kernel,
        out_shape=[jax.ShapeDtypeStruct(shape, dtype) for shape, dtype in outs],
        in_specs=specs,
        out_specs=out_specs or [VMEM] * len(outs),
        compiler_params=pltpu.CompilerParams(vmem_limit_bytes=int(mebibytes * 2**20)),
        cost_estimate=pl.CostEstimate(flops=cost, bytes_accessed=4 * 2**20, transcendentals=0),
        **more,
    )


def per_device(sections, spread, inputs, log_decay, write_proj, read_proj, grad_out):
    tokens, channels = inputs.shape
    heads = log_decay.shape[0]
    width = write_proj.shape[1]
    chunk = channels // sections
    stride = 2 * chunk + 1
    core = lax.axis_index("core").reshape(1)
    swap_cores = [(0, 1), (1, 0)]
    send, rows = call(
        functools.partial(local_kernel, sections),
        [((sections * stride, width), f32), ((24, tokens), f32)],
        [ANY] * 5,
        10**9,
        16,
        scratch_shapes=[
            pltpu.VMEM(inputs.shape, bf16),
            pltpu.VMEM(inputs.shape, bf16),
            pltpu.VMEM(write_proj.shape, bf16),
            pltpu.VMEM(write_proj.shape, bf16),
            pltpu.VMEM(log_decay.shape, f32),
            pltpu.SemaphoreType.DMA((5,)),
        ],
    )(*(in_hbm(value) for value in (inputs, grad_out, write_proj, read_proj, log_decay)))
    got = lax.all_to_all(send.reshape(sections, stride, 1, width), ("x", "zh"), 0, 0)
    got = got.reshape(sections * stride, width)

    def intra(laters):
        sizes = (
            (len(laters) * BLOCK, channels),
            ((laters[-1] + 1) * BLOCK, channels),
            ((laters[-1] + 1) * BLOCK, 2 * width),
        )
        parts = call(
            functools.partial(intra_kernel, heads, laters),
            [(size, f32) for size in sizes],
            [VMEM] * 5,
            4 * 10**9,
            52,
            out_specs=[ANY] * 3,
            scratch_shapes=[
                *(pltpu.VMEM(size, f32) for size in sizes),
                pltpu.SemaphoreType.DMA((len(laters) + 2 * (laters[-1] + 1),)),
            ],
        )(inputs, grad_out, write_proj, read_proj, rows)
        return [parts[0], in_hbm(parts[1]), in_hbm(parts[2])]

    blocks = tokens // BLOCK
    y_late, dx_late, grad_late = intra((blocks - 1,))
    y_early, dx_early, grad_early = intra(tuple(range(blocks - 1)))
    (states,) = call(
        functools.partial(scan_kernel, sections, chunk),
        [((sections, 2 * chunk, width), f32)],
        [VMEM],
        10**8,
        4,
    )(got)
    mine = lax.all_to_all(states, ("x", "zh"), 0, 0)
    keep, away = call(
        functools.partial(carry_kernel, heads, chunk, tokens // (2 * spread)),
        [((spread, tokens // (2 * spread), 2 * width), f32)] * 2,
        [SMEM] + [VMEM] * 4 + [ANY] * 2,
        10**9,
        16,
        scratch_shapes=[
            pltpu.VMEM(grad_late.shape, f32),
            pltpu.VMEM(grad_early.shape, f32),
            pltpu.SemaphoreType.DMA((2,)),
        ],
    )(core, mine, inputs, grad_out, rows, grad_late, grad_early)
    other = lax.ppermute(away, "core", swap_cores)
    parts = lax.all_to_all(keep + other, ("y", "zl"), 0, 0)
    outputs, grad_inputs = call(
        functools.partial(finish_kernel, heads, chunk),
        [((tokens, channels), bf16)] * 2,
        [VMEM] * 8,
        2 * 10**9,
        16,
    )(mine, write_proj, read_proj, rows, y_late, y_early, dx_late, dx_early)
    summed = jnp.sum(parts, axis=0)
    return (outputs, grad_inputs, summed[:, :width], summed[:, width:])


def solution(mesh, shape=(8, 4, 8, 2, 2)):
    axes = ("x", "zh", "y", "zl", "core")
    fine = Mesh(mesh.devices.reshape(shape), axes)
    seq, head = axes[:2], axes[2:]
    return jax.shard_map(
        functools.partial(per_device, shape[0] * shape[1], shape[2] * shape[3]),
        mesh=fine,
        in_specs=(P(seq, head), P(head, seq), P(seq, None), P(seq, None), P(seq, head)),
        out_specs=(P(seq, head), P(seq, head), P(axes, None), P(axes, None)),
        check_vma=False,
    )
```

```python
import functools

import jax
import jax.numpy as jnp
from jax import lax
from jax.experimental import pallas as pl
from jax.experimental.pallas import tpu as pltpu
from jax.sharding import Mesh, PartitionSpec as P

f32 = jnp.float32
bf16 = jnp.bfloat16
VMEM = pl.BlockSpec(memory_space=pltpu.VMEM)
SMEM = pl.BlockSpec(memory_space=pltpu.SMEM)
ANY = pl.BlockSpec(memory_space=pl.ANY)
BLOCK = 256
GRANT = (52, 50)


def dot(a, b, dims):
    return lax.dot_general(a, b, (dims, ((), ())), preferred_element_type=f32)


def split(value):
    high = value.astype(bf16)
    return high, (value - high.astype(f32)).astype(bf16)


def lanes_of_heads(columns, heads, width):
    tokens = columns.shape[0]
    lane = lax.broadcasted_iota(jnp.int32, (tokens, heads * width), 1) // width
    spread = jnp.broadcast_to(columns[:, 0:1], (tokens, heads * width))
    for head in range(1, heads):
        spread = jnp.where(lane == head, columns[:, head : head + 1], spread)
    return spread


def local_kernel(
    sections,
    x_hbm,
    g_hbm,
    write_hbm,
    read_hbm,
    decay_hbm,
    send_ref,
    rows_ref,
    x_ref,
    g_ref,
    write_ref,
    read_ref,
    decay_ref,
    arrived,
):
    pairs = (
        (decay_hbm, decay_ref),
        (x_hbm, x_ref),
        (write_hbm, write_ref),
        (g_hbm, g_ref),
        (read_hbm, read_ref),
    )
    copies = [
        pltpu.make_async_copy(source, target, arrived.at[at])
        for at, (source, target) in enumerate(pairs)
    ]
    for copy in copies:
        copy.start()
    heads, tokens = decay_ref.shape
    channels = x_ref.shape[1]
    head_size = channels // heads
    chunk = channels // sections
    lanes = 128
    upto = (
        lax.broadcasted_iota(jnp.int32, (lanes, lanes), 0)
        <= lax.broadcasted_iota(jnp.int32, (lanes, lanes), 1)
    ).astype(f32).astype(bf16)
    copies[0].wait()
    decay = jnp.concatenate([decay_ref[...], jnp.zeros((8 - heads, tokens), f32)], axis=0)
    first, _ = split(decay)
    second, third = split(decay - first.astype(f32))
    wide = jnp.concatenate([first.astype(f32), second.astype(f32), third.astype(f32)], axis=0)
    count = tokens // lanes
    stacked = jnp.concatenate(
        [wide[:, part * lanes : (part + 1) * lanes] for part in range(count)], axis=0
    ).astype(bf16)
    summed = dot(stacked, upto, ((1,), (0,)))
    parts = []
    before = jnp.zeros((8, 1), f32)
    for part in range(count):
        base = 24 * part
        inside = summed[base : base + 8] + summed[base + 8 : base + 16] + summed[base + 16 : base + 24]
        parts.append(inside + before)
        before = before + inside[:, lanes - 1 : lanes]
    cumul = jnp.concatenate(parts, axis=1)
    rows = jnp.concatenate([cumul, jnp.exp(cumul), jnp.exp(before - cumul)], axis=0)
    rows_ref[...] = rows
    total = jnp.exp(before)
    cols = rows.T
    per_head = head_size // chunk
    for flow, (values_ref, vectors_ref, column) in enumerate(
        ((x_ref, write_ref, 16), (g_ref, read_ref, 8))
    ):
        copies[1 + 2 * flow].wait()
        turned = values_ref[...].T
        copies[2 + 2 * flow].wait()
        vectors = vectors_ref[...].astype(f32)
        width = vectors.shape[1]
        for head in range(heads):
            state = dot(
                turned[head * head_size : (head + 1) * head_size],
                jnp.concatenate(split(vectors * cols[:, column + head : column + head + 1]), axis=1),
                ((1,), (0,)),
            )
            state = state[:, :width] + state[:, width:]
            for part in range(per_head):
                base = (head * per_head + part) * (2 * chunk + 1)
                at = base + flow * chunk
                send_ref[at : at + chunk, :] = state[part * chunk : (part + 1) * chunk]
                if flow == 0:
                    at = base + 2 * chunk
                    send_ref[at : at + 1, :] = jnp.broadcast_to(total[head : head + 1], (1, width))


def scan_kernel(sections, chunk, got_ref, out_ref):
    stride = 2 * chunk + 1

    def total(section):
        base = section * stride + 2 * chunk
        return got_ref[base : base + 1, :]

    running = jnp.zeros((chunk, got_ref.shape[1]), f32)
    for section in range(sections):
        base = section * stride
        out_ref[section, 0:chunk, :] = running
        running = total(section) * running + got_ref[base : base + chunk, :]
    running = jnp.zeros((chunk, got_ref.shape[1]), f32)
    for section in range(sections - 1, -1, -1):
        base = section * stride + chunk
        out_ref[section, chunk : 2 * chunk, :] = running
        running = total(section) * running + got_ref[base : base + chunk, :]


def intra_kernel(
    heads,
    laters,
    x_ref,
    g_ref,
    write_ref,
    read_ref,
    rows_ref,
    *rest,
):
    joins = len(rest) == 9
    if joins:
        before_hbm, y_hbm, dx_hbm, grad_ref, y_ref, dx_ref, before_ref, left, arrived = rest
        before = pltpu.make_async_copy(before_hbm, before_ref, arrived)
        before.start()
    else:
        y_hbm, dx_hbm, grad_hbm, y_ref, dx_ref, grad_ref, left = rest
    channels = x_ref.shape[1]
    head_size = channels // heads
    width = write_ref.shape[1]
    started = []

    def leave(source, target, first, count):
        at = pl.ds(first, count)
        copy = pltpu.make_async_copy(source.at[at], target.at[at], left.at[len(started)])
        copy.start()
        started.append(copy)

    cols = rows_ref[...].T
    y_ref[...] = jnp.zeros_like(y_ref)
    dx_ref[...] = jnp.zeros_like(dx_ref)
    grad_ref[...] = jnp.zeros_like(grad_ref)
    causal = lax.broadcasted_iota(jnp.int32, (BLOCK, BLOCK), 0) >= lax.broadcasted_iota(
        jnp.int32, (BLOCK, BLOCK), 1
    )
    for place, later in enumerate(laters):
        t = slice(later * BLOCK, (later + 1) * BLOCK)
        mine = slice(place * BLOCK, (place + 1) * BLOCK)
        read = read_ref[t, :]
        g_block = g_ref[t, :]
        for earlier in range(later + 1):
            j = slice(earlier * BLOCK, (earlier + 1) * BLOCK)
            write = write_ref[j, :]
            x_block = x_ref[j, :]
            scores = dot(read, write, ((1,), (1,)))
            score_grad = jnp.zeros((BLOCK, BLOCK), f32)
            for head in range(heads):
                own = slice(head * head_size, (head + 1) * head_size)
                differ = cols[t, head : head + 1] - rows_ref[head : head + 1, j]
                if later == earlier:
                    differ = jnp.where(causal, differ, -jnp.inf)
                decay = jnp.exp(differ)
                mixing = (scores * decay).astype(bf16)
                x_head = x_block[:, own]
                g_head = g_block[:, own]
                y_ref[mine, own] += dot(mixing, x_head, ((1,), (0,)))
                dx_ref[j, own] += dot(mixing, g_head, ((0,), (0,)))
                score_grad += dot(g_head, x_head, ((1,), (1,))) * decay
            high, low = split(score_grad)
            grad_ref[j, 0:width] += dot(high, read, ((0,), (0,))) + dot(low, read, ((0,), (0,)))
            grad_ref[t, width:] += dot(high, write, ((1,), (0,))) + dot(low, write, ((1,), (0,)))
            if place == len(laters) - 1:
                leave(dx_ref, dx_hbm, earlier * BLOCK, BLOCK)
                if earlier < later and not joins:
                    leave(grad_ref, grad_hbm, earlier * BLOCK, BLOCK)
        leave(y_ref, y_hbm, place * BLOCK, BLOCK)
    if joins:
        before.wait()
        grad_ref[...] += before_ref[...]
    else:
        leave(grad_ref, grad_hbm, laters[-1] * BLOCK, BLOCK)
    for copy in started:
        copy.wait()


def states_of(state_ref, chunk):
    forward = state_ref[:, 0:chunk, :]
    backward = state_ref[:, chunk:, :]
    flat = (forward.shape[0] * chunk, forward.shape[2])
    return forward.reshape(flat), backward.reshape(flat)


def carried(values, state, columns, heads):
    rows, width = state.shape
    row_head = lax.broadcasted_iota(jnp.int32, (rows, 1), 0) // (rows // heads)
    total = None
    for head in range(heads):
        mine = jnp.where(row_head == head, state, 0.0)
        product = dot(values, jnp.concatenate(split(mine), axis=1), ((1,), (0,)))
        product = (product[:, :width] + product[:, width:]) * columns[:, head : head + 1]
        total = product if total is None else total + product
    return total


def carry_kernel(
    heads,
    chunk,
    group,
    core_ref,
    state_ref,
    x_ref,
    g_ref,
    rows_ref,
    intra_ref,
    keep_ref,
    send_ref,
):
    forward, backward = states_of(state_ref, chunk)
    width = forward.shape[1]
    count = keep_ref.shape[0]
    cols = rows_ref[...].T
    of_write = carried(x_ref[...], backward, cols[:, 16:24], heads)
    of_read = carried(g_ref[...], forward, cols[:, 8:16], heads)
    whole = jnp.concatenate([of_write, of_read], axis=1) + intra_ref[...]
    whole = whole.reshape(count, 2, group, 2 * width)

    @pl.when(core_ref[0] == 0)
    def _():
        keep_ref[...] = whole[:, 0]
        send_ref[...] = whole[:, 1]

    @pl.when(core_ref[0] != 0)
    def _():
        keep_ref[...] = whole[:, 1]
        send_ref[...] = whole[:, 0]


def join_kernel(keep_ref, other_ref, out_hbm, out_ref, left):
    pieces = left.shape[0]
    count = keep_ref.shape[0] // pieces
    copies = []
    for piece in range(pieces):
        at = pl.ds(piece * count, count)
        out_ref[at] = keep_ref[at] + other_ref[at]
        copies.append(pltpu.make_async_copy(out_ref.at[at], out_hbm.at[at], left.at[piece]))
        copies[-1].start()
    for copy in copies:
        copy.wait()


def finish_kernel(
    heads,
    chunk,
    state_ref,
    write_ref,
    read_ref,
    rows_ref,
    y_late_ref,
    y_early_ref,
    dx_late_ref,
    dx_early_ref,
    out_ref,
    dout_ref,
):
    forward, backward = states_of(state_ref, chunk)
    head_size = forward.shape[0] // heads
    read, write = read_ref[...], write_ref[...]

    def inter(tokens, state):
        return dot(
            jnp.concatenate([tokens, tokens], axis=1),
            jnp.concatenate(split(state), axis=1),
            ((1,), (1,)),
        )

    known = y_early_ref.shape[0]
    cols = rows_ref[...].T
    outer = inter(read, forward) * lanes_of_heads(cols[:, 8:16], heads, head_size)
    out_ref[0:known, :] = (y_early_ref[...] + outer[:known]).astype(bf16)
    out_ref[known:, :] = (y_late_ref[...] + outer[known:]).astype(bf16)
    outer = inter(write, backward) * lanes_of_heads(cols[:, 16:24], heads, head_size)
    dout_ref[0:known, :] = (dx_late_ref[0:known, :] + dx_early_ref[...] + outer[:known]).astype(bf16)
    dout_ref[known:, :] = (dx_late_ref[known:, :] + outer[known:]).astype(bf16)


def in_hbm(value):
    return pltpu.with_memory_space_constraint(value, pltpu.HBM)


def call(kernel, outs, specs, cost, mebibytes, out_specs=None, **more):
    return pl.pallas_call(
        kernel,
        out_shape=[jax.ShapeDtypeStruct(shape, dtype) for shape, dtype in outs],
        in_specs=specs,
        out_specs=out_specs or [VMEM] * len(outs),
        compiler_params=pltpu.CompilerParams(vmem_limit_bytes=int(mebibytes * 2**20)),
        cost_estimate=pl.CostEstimate(flops=cost, bytes_accessed=4 * 2**20, transcendentals=0),
        **more,
    )


def per_device(sections, spread, inputs, log_decay, write_proj, read_proj, grad_out):
    tokens, channels = inputs.shape
    heads = log_decay.shape[0]
    width = write_proj.shape[1]
    chunk = channels // sections
    stride = 2 * chunk + 1
    core = lax.axis_index("core").reshape(1)
    swap_cores = [(0, 1), (1, 0)]
    send, rows, inputs_near, grad_near, write_near, read_near = call(
        functools.partial(local_kernel, sections),
        [
            ((sections * stride, width), f32),
            ((24, tokens), f32),
            (inputs.shape, bf16),
            (inputs.shape, bf16),
            (write_proj.shape, bf16),
            (write_proj.shape, bf16),
        ],
        [ANY] * 5,
        10**9,
        16,
        scratch_shapes=[
            pltpu.VMEM(log_decay.shape, f32),
            pltpu.SemaphoreType.DMA((5,)),
        ],
    )(*(in_hbm(value) for value in (inputs, grad_out, write_proj, read_proj, log_decay)))
    inputs, grad_out, write_proj, read_proj = inputs_near, grad_near, write_near, read_near
    got = lax.all_to_all(send.reshape(sections, stride, 1, width), ("x", "zh"), 0, 0)
    got = got.reshape(sections * stride, width)

    def intra(laters, before=None):
        joins = before is not None
        reach = (laters[-1] + 1) * BLOCK
        sizes = (
            (len(laters) * BLOCK, channels),
            (reach, channels),
            (tokens if joins else reach, 2 * width),
        )
        scratch = [pltpu.VMEM(size, f32) for size in sizes]
        copies = pltpu.SemaphoreType.DMA((len(laters) + 2 * (laters[-1] + 1),))
        scratch += [copies, pltpu.SemaphoreType.DMA(())] if joins else [copies]
        parts = call(
            functools.partial(intra_kernel, heads, laters),
            [(size, f32) for size in sizes],
            [VMEM] * 5 + [ANY] * joins,
            4 * 10**9,
            GRANT[joins],
            out_specs=[ANY, ANY, VMEM if joins else ANY],
            scratch_shapes=scratch,
        )(inputs, grad_out, write_proj, read_proj, rows, *([in_hbm(before)] if joins else []))
        return [parts[0], in_hbm(parts[1]), parts[2]]

    blocks = tokens // BLOCK
    y_late, dx_late, grad_late = intra((blocks - 1,))
    y_early, dx_early, grad_intra = intra(tuple(range(blocks - 1)), grad_late)
    (states,) = call(
        functools.partial(scan_kernel, sections, chunk),
        [((sections, 2 * chunk, width), f32)],
        [VMEM],
        10**8,
        4,
    )(got)
    mine = lax.all_to_all(states, ("x", "zh"), 0, 0)
    keep, away = call(
        functools.partial(carry_kernel, heads, chunk, tokens // (2 * spread)),
        [((spread, tokens // (2 * spread), 2 * width), f32)] * 2,
        [SMEM] + [VMEM] * 5,
        10**9,
        16,
    )(core, mine, inputs, grad_out, rows, grad_intra)
    other = lax.ppermute(away, "core", swap_cores)
    (joined,) = call(
        join_kernel,
        [(keep.shape, f32)],
        [VMEM] * 2,
        10**7,
        8,
        out_specs=[ANY],
        scratch_shapes=[pltpu.VMEM(keep.shape, f32), pltpu.SemaphoreType.DMA((2,))],
    )(keep, other)
    parts = lax.all_to_all(joined, ("y", "zl"), 0, 0)
    outputs, grad_inputs = call(
        functools.partial(finish_kernel, heads, chunk),
        [((tokens, channels), bf16)] * 2,
        [VMEM] * 8,
        2 * 10**9,
        16,
    )(mine, write_proj, read_proj, rows, y_late, y_early, dx_late, dx_early)
    summed = jnp.sum(parts, axis=0)
    return (outputs, grad_inputs, summed[:, :width], summed[:, width:])


def solution(mesh, shape=(8, 4, 8, 2, 2)):
    axes = ("x", "zh", "y", "zl", "core")
    fine = Mesh(mesh.devices.reshape(shape), axes)
    seq, head = axes[:2], axes[2:]
    return jax.shard_map(
        functools.partial(per_device, shape[0] * shape[1], shape[2] * shape[3]),
        mesh=fine,
        in_specs=(P(seq, head), P(head, seq), P(seq, None), P(seq, None), P(seq, head)),
        out_specs=(P(seq, head), P(seq, head), P(axes, None), P(axes, None)),
        check_vma=False,
    )
```

```python
import functools

import jax
import jax.numpy as jnp
from jax import lax
from jax.experimental import pallas as pl
from jax.experimental.pallas import tpu as pltpu
from jax.sharding import Mesh, PartitionSpec as P

f32 = jnp.float32
bf16 = jnp.bfloat16
VMEM = pl.BlockSpec(memory_space=pltpu.VMEM)
SMEM = pl.BlockSpec(memory_space=pltpu.SMEM)
ANY = pl.BlockSpec(memory_space=pl.ANY)
BLOCK = 256
GRANT = (52, 50)


def dot(a, b, dims):
    return lax.dot_general(a, b, (dims, ((), ())), preferred_element_type=f32)


def split(value):
    high = value.astype(bf16)
    return high, (value - high.astype(f32)).astype(bf16)


def lanes_of_heads(columns, heads, width):
    tokens = columns.shape[0]
    lane = lax.broadcasted_iota(jnp.int32, (tokens, heads * width), 1) // width
    spread = jnp.broadcast_to(columns[:, 0:1], (tokens, heads * width))
    for head in range(1, heads):
        spread = jnp.where(lane == head, columns[:, head : head + 1], spread)
    return spread


def local_kernel(
    sections,
    x_hbm,
    g_hbm,
    write_hbm,
    read_hbm,
    decay_hbm,
    send_hbm,
    rows_ref,
    x_ref,
    g_ref,
    write_ref,
    read_ref,
    decay_ref,
    arrived,
    send_ref,
    left,
):
    pairs = (
        (decay_hbm, decay_ref),
        (x_hbm, x_ref),
        (write_hbm, write_ref),
        (g_hbm, g_ref),
        (read_hbm, read_ref),
    )
    copies = [
        pltpu.make_async_copy(source, target, arrived.at[at])
        for at, (source, target) in enumerate(pairs)
    ]
    for copy in copies:
        copy.start()
    heads, tokens = decay_ref.shape
    channels = x_ref.shape[1]
    head_size = channels // heads
    chunk = channels // sections
    lanes = 128
    upto = (
        lax.broadcasted_iota(jnp.int32, (lanes, lanes), 0)
        <= lax.broadcasted_iota(jnp.int32, (lanes, lanes), 1)
    ).astype(f32).astype(bf16)
    copies[0].wait()
    decay = jnp.concatenate([decay_ref[...], jnp.zeros((8 - heads, tokens), f32)], axis=0)
    first, _ = split(decay)
    second, third = split(decay - first.astype(f32))
    wide = jnp.concatenate([first.astype(f32), second.astype(f32), third.astype(f32)], axis=0)
    count = tokens // lanes
    stacked = jnp.concatenate(
        [wide[:, part * lanes : (part + 1) * lanes] for part in range(count)], axis=0
    ).astype(bf16)
    summed = dot(stacked, upto, ((1,), (0,)))
    parts = []
    before = jnp.zeros((8, 1), f32)
    for part in range(count):
        base = 24 * part
        inside = summed[base : base + 8] + summed[base + 8 : base + 16] + summed[base + 16 : base + 24]
        parts.append(inside + before)
        before = before + inside[:, lanes - 1 : lanes]
    cumul = jnp.concatenate(parts, axis=1)
    rows = jnp.concatenate([cumul, jnp.exp(cumul), jnp.exp(before - cumul)], axis=0)
    rows_ref[...] = rows
    total = jnp.exp(before)
    cols = rows.T
    per_head = head_size // chunk
    for flow, (values_ref, vectors_ref, column) in enumerate(
        ((x_ref, write_ref, 16), (g_ref, read_ref, 8))
    ):
        copies[1 + 2 * flow].wait()
        turned = values_ref[...].T
        copies[2 + 2 * flow].wait()
        vectors = vectors_ref[...].astype(f32)
        width = vectors.shape[1]
        for head in range(heads):
            state = dot(
                turned[head * head_size : (head + 1) * head_size],
                jnp.concatenate(split(vectors * cols[:, column + head : column + head + 1]), axis=1),
                ((1,), (0,)),
            )
            state = state[:, :width] + state[:, width:]
            for part in range(per_head):
                base = (head * per_head + part) * (2 * chunk + 1)
                at = base + flow * chunk
                send_ref[at : at + chunk, :] = state[part * chunk : (part + 1) * chunk]
                if flow == 0:
                    at = base + 2 * chunk
                    send_ref[at : at + 1, :] = jnp.broadcast_to(total[head : head + 1], (1, width))
            if flow == 1:
                count = per_head * (2 * chunk + 1)
                at = pl.ds(head * count, count)
                leaving = pltpu.make_async_copy(send_ref.at[at], send_hbm.at[at], left.at[head])
                leaving.start()
                copies.append(leaving)
    for copy in copies[len(pairs) :]:
        copy.wait()


def scan_kernel(sections, chunk, got_ref, out_ref):
    stride = 2 * chunk + 1

    def total(section):
        base = section * stride + 2 * chunk
        return got_ref[base : base + 1, :]

    running = jnp.zeros((chunk, got_ref.shape[1]), f32)
    for section in range(sections):
        base = section * stride
        out_ref[section, 0:chunk, :] = running
        running = total(section) * running + got_ref[base : base + chunk, :]
    running = jnp.zeros((chunk, got_ref.shape[1]), f32)
    for section in range(sections - 1, -1, -1):
        base = section * stride + chunk
        out_ref[section, chunk : 2 * chunk, :] = running
        running = total(section) * running + got_ref[base : base + chunk, :]


def intra_kernel(
    heads,
    laters,
    x_ref,
    g_ref,
    write_ref,
    read_ref,
    rows_ref,
    *rest,
):
    joins = len(rest) == 9
    if joins:
        before_hbm, y_hbm, dx_hbm, grad_ref, y_ref, dx_ref, before_ref, left, arrived = rest
        before = pltpu.make_async_copy(before_hbm, before_ref, arrived)
        before.start()
    else:
        y_hbm, dx_hbm, grad_hbm, y_ref, dx_ref, grad_ref, left = rest
    channels = x_ref.shape[1]
    head_size = channels // heads
    width = write_ref.shape[1]
    started = []

    def leave(source, target, first, count):
        at = pl.ds(first, count)
        copy = pltpu.make_async_copy(source.at[at], target.at[at], left.at[len(started)])
        copy.start()
        started.append(copy)

    cols = rows_ref[...].T
    y_ref[...] = jnp.zeros_like(y_ref)
    dx_ref[...] = jnp.zeros_like(dx_ref)
    grad_ref[...] = jnp.zeros_like(grad_ref)
    causal = lax.broadcasted_iota(jnp.int32, (BLOCK, BLOCK), 0) >= lax.broadcasted_iota(
        jnp.int32, (BLOCK, BLOCK), 1
    )
    for place, later in enumerate(laters):
        t = slice(later * BLOCK, (later + 1) * BLOCK)
        mine = slice(place * BLOCK, (place + 1) * BLOCK)
        read = read_ref[t, :]
        g_block = g_ref[t, :]
        for earlier in range(later + 1):
            j = slice(earlier * BLOCK, (earlier + 1) * BLOCK)
            write = write_ref[j, :]
            x_block = x_ref[j, :]
            scores = dot(read, write, ((1,), (1,)))
            score_grad = jnp.zeros((BLOCK, BLOCK), f32)
            for head in range(heads):
                own = slice(head * head_size, (head + 1) * head_size)
                differ = cols[t, head : head + 1] - rows_ref[head : head + 1, j]
                if later == earlier:
                    differ = jnp.where(causal, differ, -jnp.inf)
                decay = jnp.exp(differ)
                mixing = (scores * decay).astype(bf16)
                x_head = x_block[:, own]
                g_head = g_block[:, own]
                y_ref[mine, own] += dot(mixing, x_head, ((1,), (0,)))
                dx_ref[j, own] += dot(mixing, g_head, ((0,), (0,)))
                score_grad += dot(g_head, x_head, ((1,), (1,))) * decay
            high, low = split(score_grad)
            grad_ref[j, 0:width] += dot(high, read, ((0,), (0,))) + dot(low, read, ((0,), (0,)))
            grad_ref[t, width:] += dot(high, write, ((1,), (0,))) + dot(low, write, ((1,), (0,)))
            if place == len(laters) - 1:
                leave(dx_ref, dx_hbm, earlier * BLOCK, BLOCK)
                if earlier < later and not joins:
                    leave(grad_ref, grad_hbm, earlier * BLOCK, BLOCK)
        leave(y_ref, y_hbm, place * BLOCK, BLOCK)
    if joins:
        before.wait()
        grad_ref[...] += before_ref[...]
    else:
        leave(grad_ref, grad_hbm, laters[-1] * BLOCK, BLOCK)
    for copy in started:
        copy.wait()


def states_of(state_ref, chunk):
    forward = state_ref[:, 0:chunk, :]
    backward = state_ref[:, chunk:, :]
    flat = (forward.shape[0] * chunk, forward.shape[2])
    return forward.reshape(flat), backward.reshape(flat)


def carried(values, state, columns, heads):
    rows, width = state.shape
    row_head = lax.broadcasted_iota(jnp.int32, (rows, 1), 0) // (rows // heads)
    total = None
    for head in range(heads):
        mine = jnp.where(row_head == head, state, 0.0)
        product = dot(values, jnp.concatenate(split(mine), axis=1), ((1,), (0,)))
        product = (product[:, :width] + product[:, width:]) * columns[:, head : head + 1]
        total = product if total is None else total + product
    return total


def carry_kernel(
    heads,
    chunk,
    group,
    core_ref,
    state_ref,
    x_ref,
    g_ref,
    rows_ref,
    intra_ref,
    keep_ref,
    send_ref,
):
    forward, backward = states_of(state_ref, chunk)
    width = forward.shape[1]
    count = keep_ref.shape[0]
    cols = rows_ref[...].T
    of_write = carried(x_ref[...], backward, cols[:, 16:24], heads)
    of_read = carried(g_ref[...], forward, cols[:, 8:16], heads)
    whole = jnp.concatenate([of_write, of_read], axis=1) + intra_ref[...]
    whole = whole.reshape(count, 2, group, 2 * width)

    @pl.when(core_ref[0] == 0)
    def _():
        keep_ref[...] = whole[:, 0]
        send_ref[...] = whole[:, 1]

    @pl.when(core_ref[0] != 0)
    def _():
        keep_ref[...] = whole[:, 1]
        send_ref[...] = whole[:, 0]


def join_kernel(keep_ref, other_ref, out_hbm, out_ref, left):
    pieces = left.shape[0]
    count = keep_ref.shape[0] // pieces
    copies = []
    for piece in range(pieces):
        at = pl.ds(piece * count, count)
        out_ref[at] = keep_ref[at] + other_ref[at]
        copies.append(pltpu.make_async_copy(out_ref.at[at], out_hbm.at[at], left.at[piece]))
        copies[-1].start()
    for copy in copies:
        copy.wait()


def finish_kernel(
    heads,
    chunk,
    state_ref,
    write_ref,
    read_ref,
    rows_ref,
    y_late_ref,
    y_early_ref,
    dx_late_ref,
    dx_early_ref,
    out_ref,
    dout_ref,
):
    forward, backward = states_of(state_ref, chunk)
    head_size = forward.shape[0] // heads
    read, write = read_ref[...], write_ref[...]

    def inter(tokens, state):
        return dot(
            jnp.concatenate([tokens, tokens], axis=1),
            jnp.concatenate(split(state), axis=1),
            ((1,), (1,)),
        )

    known = y_early_ref.shape[0]
    cols = rows_ref[...].T
    outer = inter(read, forward) * lanes_of_heads(cols[:, 8:16], heads, head_size)
    out_ref[0:known, :] = (y_early_ref[...] + outer[:known]).astype(bf16)
    out_ref[known:, :] = (y_late_ref[...] + outer[known:]).astype(bf16)
    outer = inter(write, backward) * lanes_of_heads(cols[:, 16:24], heads, head_size)
    dout_ref[0:known, :] = (dx_late_ref[0:known, :] + dx_early_ref[...] + outer[:known]).astype(bf16)
    dout_ref[known:, :] = (dx_late_ref[known:, :] + outer[known:]).astype(bf16)


def in_hbm(value):
    return pltpu.with_memory_space_constraint(value, pltpu.HBM)


def call(kernel, outs, specs, cost, mebibytes, out_specs=None, **more):
    return pl.pallas_call(
        kernel,
        out_shape=[jax.ShapeDtypeStruct(shape, dtype) for shape, dtype in outs],
        in_specs=specs,
        out_specs=out_specs or [VMEM] * len(outs),
        compiler_params=pltpu.CompilerParams(vmem_limit_bytes=int(mebibytes * 2**20)),
        cost_estimate=pl.CostEstimate(flops=cost, bytes_accessed=4 * 2**20, transcendentals=0),
        **more,
    )


def per_device(sections, spread, inputs, log_decay, write_proj, read_proj, grad_out):
    tokens, channels = inputs.shape
    heads = log_decay.shape[0]
    width = write_proj.shape[1]
    chunk = channels // sections
    stride = 2 * chunk + 1
    core = lax.axis_index("core").reshape(1)
    swap_cores = [(0, 1), (1, 0)]
    send, rows, inputs_near, grad_near, write_near, read_near = call(
        functools.partial(local_kernel, sections),
        [
            ((sections * stride, width), f32),
            ((24, tokens), f32),
            (inputs.shape, bf16),
            (inputs.shape, bf16),
            (write_proj.shape, bf16),
            (write_proj.shape, bf16),
        ],
        [ANY] * 5,
        10**9,
        16,
        scratch_shapes=[
            pltpu.VMEM(log_decay.shape, f32),
            pltpu.SemaphoreType.DMA((5,)),
            pltpu.VMEM((sections * stride, width), f32),
            pltpu.SemaphoreType.DMA((heads,)),
        ],
        out_specs=[ANY] + [VMEM] * 5,
    )(*(in_hbm(value) for value in (inputs, grad_out, write_proj, read_proj, log_decay)))
    inputs, grad_out, write_proj, read_proj = inputs_near, grad_near, write_near, read_near
    got = lax.all_to_all(send.reshape(sections, stride, 1, width), ("x", "zh"), 0, 0)
    got = got.reshape(sections * stride, width)

    def intra(laters, before=None):
        joins = before is not None
        reach = (laters[-1] + 1) * BLOCK
        sizes = (
            (len(laters) * BLOCK, channels),
            (reach, channels),
            (tokens if joins else reach, 2 * width),
        )
        scratch = [pltpu.VMEM(size, f32) for size in sizes]
        copies = pltpu.SemaphoreType.DMA((len(laters) + 2 * (laters[-1] + 1),))
        scratch += [copies, pltpu.SemaphoreType.DMA(())] if joins else [copies]
        parts = call(
            functools.partial(intra_kernel, heads, laters),
            [(size, f32) for size in sizes],
            [VMEM] * 5 + [ANY] * joins,
            4 * 10**9,
            GRANT[joins],
            out_specs=[ANY, ANY, VMEM if joins else ANY],
            scratch_shapes=scratch,
        )(inputs, grad_out, write_proj, read_proj, rows, *([in_hbm(before)] if joins else []))
        return [parts[0], in_hbm(parts[1]), parts[2]]

    blocks = tokens // BLOCK
    y_late, dx_late, grad_late = intra((blocks - 1,))
    y_early, dx_early, grad_intra = intra(tuple(range(blocks - 1)), grad_late)
    (states,) = call(
        functools.partial(scan_kernel, sections, chunk),
        [((sections, 2 * chunk, width), f32)],
        [VMEM],
        10**8,
        4,
    )(got)
    mine = lax.all_to_all(states, ("x", "zh"), 0, 0)
    keep, away = call(
        functools.partial(carry_kernel, heads, chunk, tokens // (2 * spread)),
        [((spread, tokens // (2 * spread), 2 * width), f32)] * 2,
        [SMEM] + [VMEM] * 5,
        10**9,
        16,
    )(core, mine, inputs, grad_out, rows, grad_intra)
    other = lax.ppermute(away, "core", swap_cores)
    (joined,) = call(
        join_kernel,
        [(keep.shape, f32)],
        [VMEM] * 2,
        10**7,
        8,
        out_specs=[ANY],
        scratch_shapes=[pltpu.VMEM(keep.shape, f32), pltpu.SemaphoreType.DMA((2,))],
    )(keep, other)
    parts = lax.all_to_all(joined, ("y", "zl"), 0, 0)
    outputs, grad_inputs = call(
        functools.partial(finish_kernel, heads, chunk),
        [((tokens, channels), bf16)] * 2,
        [VMEM] * 8,
        2 * 10**9,
        16,
    )(mine, write_proj, read_proj, rows, y_late, y_early, dx_late, dx_early)
    summed = jnp.sum(parts, axis=0)
    return (outputs, grad_inputs, summed[:, :width], summed[:, width:])


def solution(mesh, shape=(8, 4, 8, 2, 2)):
    axes = ("x", "zh", "y", "zl", "core")
    fine = Mesh(mesh.devices.reshape(shape), axes)
    seq, head = axes[:2], axes[2:]
    return jax.shard_map(
        functools.partial(per_device, shape[0] * shape[1], shape[2] * shape[3]),
        mesh=fine,
        in_specs=(P(seq, head), P(head, seq), P(seq, None), P(seq, None), P(seq, head)),
        out_specs=(P(seq, head), P(seq, head), P(axes, None), P(axes, None)),
        check_vma=False,
    )
```
